32 devices in a mesh: fsdp: 8 (over y, x, core), tp: 4 (over z).
Axes of the slice: x: 2, y: 2, z: 4, core: 2. Of those that a mesh axis runs over, the one named last changes fastest.
Arguments:
- inputs: bfloat16 [2, 16384, 1024], P(None, ('fsdp', 'tp')), may hold values from -6 to 6
- w_query: bfloat16 [1024, 1024], P('fsdp', 'tp'), may hold values from -0.1875 to 0.1875
- w_key: bfloat16 [1024, 1024], P('fsdp', 'tp'), may hold values from -0.375 to 0.375
- w_value: bfloat16 [1024, 1024], P('fsdp', 'tp'), may hold values from -0.1875 to 0.1875
- b_query: bfloat16 [4, 256], P('tp', 'fsdp'), may hold values from -3 to 3
- b_value: bfloat16 [4, 256], P('tp', 'fsdp'), may hold values from -0.59765625 to 0.59765625
- w_output: bfloat16 [1024, 1024], P('tp', 'fsdp'), may hold values from -0.75 to 0.75
- b_output: bfloat16 [1024], P(('fsdp', 'tp')), may hold values from -1.796875 to 1.796875
- attn_gain: bfloat16 [1024], P(('fsdp', 'tp')), may hold values from 0.25 to 1.75
- attn_shift: bfloat16 [1024], P(('fsdp', 'tp')), may hold values from -1.796875 to 1.796875
- w_up: bfloat16 [1024, 4096], P('fsdp', 'tp'), may hold values from -0.1875 to 0.1875
- b_up: bfloat16 [4, 1024], P('tp', 'fsdp'), may hold values from -3 to 3
- w_down: bfloat16 [4096, 1024], P('tp', 'fsdp'), may hold values from -0.09375 to 0.09375
- b_down: bfloat16 [1024], P(('fsdp', 'tp')), may hold values from -1.796875 to 1.796875
- mlp_gain: bfloat16 [1024], P(('fsdp', 'tp')), may hold values from 0.25 to 1.75
- mlp_shift: bfloat16 [1024], P(('fsdp', 'tp')), may hold values from -1.796875 to 1.796875
- doc_lengths: int32 [2, 8, 8], P(None, 'fsdp'), may hold values from 1 to 1536, 2048 in all within a row
- out_grad: bfloat16 [2, 16384, 1024], P(None, ('fsdp', 'tp')), may hold values from -6 to 6
Outputs:
- layer_out: bfloat16 [2, 16384, 1024], P(None, ('fsdp', 'tp'))
- input_grad: bfloat16 [2, 16384, 1024], P(None, ('fsdp', 'tp'))
- grad_w_query: float32 [1024, 1024], P('fsdp', 'tp')
- grad_w_key: float32 [1024, 1024], P('fsdp', 'tp')
- grad_w_value: float32 [1024, 1024], P('fsdp', 'tp')
- grad_b_query: float32 [4, 256], P('tp', 'fsdp')
- grad_b_value: float32 [4, 256], P('tp', 'fsdp')
- grad_w_output: float32 [1024, 1024], P('tp', 'fsdp')
- grad_b_output: float32 [1024], P(('fsdp', 'tp'))
- grad_attn_gain: float32 [1024], P(('fsdp', 'tp'))
- grad_attn_shift: float32 [1024], P(('fsdp', 'tp'))
- grad_w_up: float32 [1024, 4096], P('fsdp', 'tp')
- grad_b_up: float32 [4, 1024], P('tp', 'fsdp')
- grad_w_down: float32 [4096, 1024], P('tp', 'fsdp')
- grad_b_down: float32 [1024], P(('fsdp', 'tp'))
- grad_mlp_gain: float32 [1024], P(('fsdp', 'tp'))
- grad_mlp_shift: float32 [1024], P(('fsdp', 'tp'))
The draws below stay inside these ranges and needn't reach their ends.
Inputs may be any that keep to these rules, and one draw needn't show every extreme that they name: `doc_lengths`: each sequence's 8 lengths sum to 2048, and its longest document has exactly 1536 tokens.
All inputs are finite; a program needn't handle non-finite values.
Results may differ from the reference program's by a relative error of at most 0.02.
Values may be sent and summed in bfloat16 or wider, within the bound.
No kernel may reach another device: no remote copies, remote signals or barrier semaphores. Data moves between devices by JAX's collectives and lax.ppermute only.
A program may use at most 512 MiB of HBM per device.

```python
import math
import jax
import jax.numpy as jnp
import numpy as np
from jax import lax

D = 1024
HEADS = 16
HEAD_DIM = 64
FF = 4096
SEQ = 2048
WINDOW = 1024
DOCS = 8
MICRO = 2
TOKENS = 16384
N_FSDP = 8
N_TP = 4


def block_scale(rng, shape, cuts, least, top_value):
    loudness, own = 1.0, jax.random.fold_in(rng, 6)
    for position, shards_of in cuts:
        steps = jnp.exp(jax.random.uniform(jax.random.fold_in(own, position), (shards_of,), jnp.float32, least / len(cuts), top_value / len(cuts)))
        loudness = loudness * jnp.repeat(steps, shape[position] // shards_of).reshape([-1 if axis == position else 1 for axis in range(len(shape))])
    return loudness


def length_profile(count, total, reach, skew):
    loads = [(1 << 20) // math.isqrt(rank ** skew) + 1 for rank in range(2, count + 1)]
    spare, counts = total - reach - (count - 1), [1] * (count - 1)
    while spare > 0:
        movable = [i for i in range(count - 1) if counts[i] < reach]
        whole, budget = sum([loads[i] for i in movable]), spare
        for i in movable:
            more = min(reach - counts[i], max(1, budget * loads[i] // whole), spare)
            counts[i] = counts[i] + more
            spare = spare - more
    return np.array([reach] + counts)


def ragged(own_key, amount, total, reach, skew):
    if amount == 2:
        one = jax.random.randint(own_key, (), max(1, total - reach), min(reach, total - 1) + 1)
        return jnp.stack([one, total - one])
    sizes = jnp.asarray(length_profile(amount, total, reach, skew), jnp.int32)
    twos = (amount - 1) // 2
    donor, receiver = sizes[1:1 + 2 * twos:2], sizes[2:2 + 2 * twos:2]
    slack = jnp.minimum(donor - 1, reach - receiver)
    passed = jax.random.randint(jax.random.fold_in(own_key, 1), (twos,), 0, 1 << 20) % (slack + 1)
    sizes = sizes.at[1:1 + 2 * twos:2].set(donor - passed).at[2:2 + 2 * twos:2].set(receiver + passed)
    return sizes[jax.random.permutation(jax.random.fold_in(own_key, 2), amount)]


def scatter_about(rng, shape, spread, reach, shards=(), kind=jnp.bfloat16):
    factor_of = block_scale(rng, shape, shards, -0.22, 0.18) if shards else 1.0
    array = jax.random.normal(rng, shape, jnp.float32) * spread * factor_of
    return jnp.minimum(jnp.maximum(array, -reach), reach).astype(kind)


def setup_inputs(seed: int = 0) -> dict:
    arg_keys = jax.random.split(jax.random.key(seed), 19)
    return {
        "inputs": scatter_about(arg_keys[0], (MICRO, TOKENS, D), 1.0, 6.0, ((1, 32),)),
        "w_query": scatter_about(arg_keys[1], (D, D), D ** -0.5, 0.1875, ((0, 8), (1, 4))),
        "w_key": scatter_about(arg_keys[2], (D, D), (D // 4) ** -0.5, 0.375, ((0, 8), (1, 4))),
        "w_value": scatter_about(arg_keys[3], (D, D), D ** -0.5, 0.1875, ((0, 8), (1, 4))),
        "b_query": scatter_about(arg_keys[4], (N_TP, D // N_TP), 0.5, 3.0, ((0, 4), (1, 8))),
        "b_value": scatter_about(arg_keys[5], (N_TP, D // N_TP), 0.1, 0.59765625, ((0, 4), (1, 8))),
        "w_output": scatter_about(arg_keys[6], (D, D), (D // 16) ** -0.5, 0.75, ((0, 4), (1, 8))),
        "b_output": scatter_about(arg_keys[7], (D,), 0.3, 1.796875, ((0, 32),)),
        "attn_gain": jnp.clip(1.0 + 0.15 * jax.random.normal(arg_keys[8], (D,), jnp.float32), 0.25, 1.75).astype(jnp.bfloat16),
        "attn_shift": scatter_about(arg_keys[9], (D,), 0.3, 1.796875, ((0, 32),)),
        "w_up": scatter_about(arg_keys[10], (D, FF), D ** -0.5, 0.1875, ((0, 8), (1, 4))),
        "b_up": scatter_about(arg_keys[11], (N_TP, FF // N_TP), 0.5, 3.0, ((0, 4), (1, 8))),
        "w_down": scatter_about(arg_keys[12], (FF, D), FF ** -0.5, 0.09375, ((0, 4), (1, 8))),
        "b_down": scatter_about(arg_keys[13], (D,), 0.3, 1.796875, ((0, 32),)),
        "mlp_gain": jnp.clip(1.0 + 0.15 * jax.random.normal(arg_keys[14], (D,), jnp.float32), 0.25, 1.75).astype(jnp.bfloat16),
        "mlp_shift": scatter_about(arg_keys[15], (D,), 0.3, 1.796875, ((0, 32),)),
        "doc_lengths": jax.vmap(lambda own: ragged(own, DOCS, SEQ, SEQ * 3 // 4, 2))(jax.random.split(arg_keys[16], MICRO * N_FSDP)).reshape((MICRO, N_FSDP, DOCS)).astype(jnp.int32),
        "out_grad": scatter_about(arg_keys[17], (MICRO, TOKENS, D), 1.0, 6.0, ((1, 32),)),
    }


EPSILON = 1e-12
MASKED = -1000000000.0

@jax.custom_vjp
def low(v):
    return lax.optimization_barrier(v.astype(jnp.bfloat16)).astype(jnp.float32)

@jax.custom_vjp
def low_back(v):
    return v

def low_keep(v):
    return (low(v), None)

def low_pass(kept, grad):
    return (grad,)

def back_keep(v):
    return (v, None)

def back_low(kept, grad):
    return (low(grad),)
low.defvjp(low_keep, low_pass)
low_back.defvjp(back_keep, back_low)

def matmul(left, right):
    return jnp.dot(left, right, precision=lax.Precision.HIGHEST)

def layer_norm(values, norm_gain, norm_bias):
    average = lax.optimization_barrier(jnp.mean(values, axis=-1, keepdims=True))
    centred = values - average
    variance = lax.optimization_barrier(jnp.mean(centred * centred, axis=-1, keepdims=True))
    return centred * lax.rsqrt(variance + EPSILON) * norm_gain + norm_bias

def attend_block(query_block, seg_block, place_block, key_rows, value_rows, segments, places):
    row_count = query_block.shape[0]
    query_heads = query_block.reshape(row_count, HEADS, HEAD_DIM)
    key_heads = key_rows.reshape(SEQ, HEADS, HEAD_DIM)
    value_heads = value_rows.reshape(SEQ, HEADS, HEAD_DIM)
    scores = jnp.einsum('qhd,khd->hqk', query_heads, key_heads, precision=lax.Precision.HIGHEST) * HEAD_DIM ** (-0.5)
    scores = low_back(scores)
    allowed = (seg_block[:, None] == segments[None, :]) & (jnp.abs(place_block[:, None] - places[None, :]) < WINDOW)
    scores = jnp.where(allowed[None], scores, MASKED)
    attn_probs = low(jax.nn.softmax(scores, axis=-1))
    context = jnp.einsum('hqk,khd->qhd', attn_probs, value_heads, precision=lax.Precision.HIGHEST)
    return context.reshape(row_count, D)

def layer(tokens, w_query, w_key, w_value, b_query, b_value, w_output, b_output, attn_gain, attn_shift, w_up, b_up, w_down, b_down, mlp_gain, mlp_shift, segments, places):
    query_rows = low_back(low(matmul(tokens, w_query) + b_query))
    key_rows = low_back(low(matmul(tokens, w_key)))
    value_rows = low_back(low(matmul(tokens, w_value) + b_value))
    block_rows = min(512, SEQ)
    block_count = SEQ // block_rows
    checked = jax.checkpoint(attend_block)

    def one_block(block_item):
        return checked(block_item[0], block_item[1], block_item[2], key_rows, value_rows, segments, places)
    context = lax.map(one_block, (query_rows.reshape(block_count, block_rows, D), segments.reshape(block_count, block_rows), places.reshape(block_count, block_rows)))
    context = low_back(low(context.reshape(SEQ, D)))
    attended = low_back(matmul(context, w_output))
    hidden = low(layer_norm(tokens + attended + b_output, attn_gain, attn_shift))
    up_pre = low_back(matmul(hidden, w_up) + b_up)
    activated = low(jax.nn.gelu(up_pre, approximate=True))
    mixed = low_back(matmul(activated, w_down))
    return layer_norm(hidden + mixed + b_down, mlp_gain, mlp_shift)

def reference(inputs, w_query, w_key, w_value, b_query, b_value, w_output, b_output, attn_gain, attn_shift, w_up, b_up, w_down, b_down, mlp_gain, mlp_shift, doc_lengths, out_grad):
    weight_set = tuple((item.astype(jnp.float32) for item in (w_query, w_key, w_value, b_query.reshape(D), b_value.reshape(D), w_output, b_output, attn_gain, attn_shift, w_up, b_up.reshape(FF), w_down, b_down, mlp_gain, mlp_shift)))
    seq_count = MICRO * N_FSDP
    tokens_all = inputs.astype(jnp.float32).reshape(seq_count, SEQ, D)
    upstream_all = out_grad.astype(jnp.float32).reshape(seq_count, SEQ, D)
    lengths_all = doc_lengths.reshape(seq_count, DOCS).astype(jnp.int32)
    places = jnp.arange(SEQ, dtype=jnp.int32)

    def scan_step(totals, seq_item):
        tokens, upstream, lengths = seq_item
        doc_ends = jnp.cumsum(lengths).astype(jnp.int32)
        segments = lax.optimization_barrier(jnp.sum((places[:, None] >= doc_ends[None, :]).astype(jnp.int32), axis=1)).astype(jnp.int32)

        def forward(token_rows, *weight_args):
            return layer(token_rows, *weight_args, segments, places)
        result, pullback = jax.vjp(forward, tokens, *weight_set)
        gradients = pullback(upstream)
        new_totals = tuple((left + right for left, right in zip(totals, gradients[1:])))
        return (new_totals, (result.astype(jnp.bfloat16), gradients[0].astype(jnp.bfloat16)))
    zero_grads = tuple((jnp.zeros_like(item) for item in weight_set))
    totals, (results, token_grads) = lax.scan(scan_step, zero_grads, (tokens_all, upstream_all, lengths_all))
    layer_out = results.reshape(MICRO, N_FSDP * SEQ, D)
    input_grad = token_grads.reshape(MICRO, N_FSDP * SEQ, D)
    return (layer_out, input_grad, totals[0], totals[1], totals[2], totals[3].reshape(N_TP, D // N_TP), totals[4].reshape(N_TP, D // N_TP), totals[5], totals[6], totals[7], totals[8], totals[9], totals[10].reshape(N_TP, FF // N_TP), totals[11], totals[12], totals[13], totals[14])
```

```python
from functools import partial

import jax
import jax.numpy as jnp
from jax import lax
from jax.experimental import pallas as pl
from jax.experimental.pallas import tpu as pltpu
from jax.sharding import PartitionSpec as P

HEAD_DIM = 64
WINDOW = 1024


EPSILON = 1e-12
MASKED = -1000000000.0


def norm_forward(values, norm_gain, norm_bias):
    average = jnp.mean(values, axis=-1, keepdims=True)
    centred = values - average
    inverse = lax.rsqrt(jnp.mean(centred * centred, axis=-1, keepdims=True) + EPSILON)
    normed = centred * inverse
    return (normed * norm_gain + norm_bias, normed, inverse)


def norm_backward(upstream, normed, inverse, norm_gain):
    scaled = upstream * norm_gain
    inner_mean = jnp.mean(scaled, axis=-1, keepdims=True)
    cross_mean = jnp.mean(scaled * normed, axis=-1, keepdims=True)
    values_grad = inverse * (scaled - inner_mean - normed * cross_mean)
    return (values_grad, jnp.sum(upstream * normed, axis=0), jnp.sum(upstream, axis=0))


def segment_ids(lengths, seq_len):
    doc_ends = jnp.cumsum(lengths)
    places = jnp.arange(seq_len, dtype=jnp.int32)
    segments = jnp.sum((places[:, None] >= doc_ends[None, :]).astype(jnp.int32), axis=1)
    return (segments, places)


def block_scores(query_heads, key_heads, segments, places, row_start, block_rows):
    seg_rows = segments[row_start : row_start + block_rows]
    place_rows = places[row_start : row_start + block_rows]
    allowed = (seg_rows[:, None] == segments[None, :]) & (
        jnp.abs(place_rows[:, None] - places[None, :]) < WINDOW
    )
    scores = jnp.einsum(
        "qhd,khd->hqk", query_heads, key_heads, preferred_element_type=jnp.float32
    ) * HEAD_DIM ** (-0.5)
    return jnp.where(allowed[None], scores, MASKED)


def attention_forward(query_rows, key_rows, value_rows, segments, places):
    seq_len, col_count = query_rows.shape
    head_count = col_count // HEAD_DIM
    block_rows = min(512, seq_len)
    key_heads = key_rows.reshape(seq_len, head_count, HEAD_DIM)
    value_heads = value_rows.reshape(seq_len, head_count, HEAD_DIM)
    outputs = []
    logsums = []
    for row_start in range(0, seq_len, block_rows):
        query_heads = query_rows[row_start : row_start + block_rows].reshape(
            block_rows, head_count, HEAD_DIM
        )
        scores = block_scores(query_heads, key_heads, segments, places, row_start, block_rows)
        row_top = jnp.max(scores, axis=-1, keepdims=True)
        exponent = jnp.exp(scores - row_top)
        row_total = jnp.sum(exponent, axis=-1, keepdims=True)
        attn_probs = (exponent / row_total).astype(jnp.bfloat16)
        context = jnp.einsum(
            "hqk,khd->qhd", attn_probs, value_heads, preferred_element_type=jnp.float32
        )
        outputs.append(context.reshape(block_rows, col_count))
        logsums.append(row_top + jnp.log(row_total))
    return (jnp.concatenate(outputs, axis=0).astype(jnp.bfloat16), jnp.concatenate(logsums, axis=1))


def attention_backward(query_rows, key_rows, value_rows, context_grad, logsums, segments, places):
    seq_len, col_count = query_rows.shape
    head_count = col_count // HEAD_DIM
    score_scale = HEAD_DIM ** (-0.5)
    block_rows = min(512, seq_len)
    key_heads = key_rows.reshape(seq_len, head_count, HEAD_DIM)
    value_heads = value_rows.reshape(seq_len, head_count, HEAD_DIM)
    key_grad = jnp.zeros((seq_len, head_count, HEAD_DIM), jnp.float32)
    value_grad = jnp.zeros((seq_len, head_count, HEAD_DIM), jnp.float32)
    query_parts = []
    for row_start in range(0, seq_len, block_rows):
        query_heads = query_rows[row_start : row_start + block_rows].reshape(
            block_rows, head_count, HEAD_DIM
        )
        grad_heads = context_grad[row_start : row_start + block_rows].reshape(
            block_rows, head_count, HEAD_DIM
        )
        scores = block_scores(query_heads, key_heads, segments, places, row_start, block_rows)
        attn_probs = jnp.exp(scores - logsums[:, row_start : row_start + block_rows])
        value_grad = value_grad + jnp.einsum(
            "hqk,qhd->khd",
            attn_probs.astype(jnp.bfloat16),
            grad_heads,
            preferred_element_type=jnp.float32,
        )
        prob_grad = jnp.einsum(
            "qhd,khd->hqk", grad_heads, value_heads, preferred_element_type=jnp.float32
        )
        row_delta = jnp.sum(attn_probs * prob_grad, axis=-1, keepdims=True)
        score_grad = (attn_probs * (prob_grad - row_delta)).astype(jnp.bfloat16)
        query_part = (
            jnp.einsum("hqk,khd->qhd", score_grad, key_heads, preferred_element_type=jnp.float32)
            * score_scale
        )
        query_parts.append(query_part.astype(jnp.bfloat16).reshape(block_rows, col_count))
        key_grad = (
            key_grad
            + jnp.einsum(
                "hqk,qhd->khd", score_grad, query_heads, preferred_element_type=jnp.float32
            )
            * score_scale
        )
    query_grad = jnp.concatenate(query_parts, axis=0)
    return (
        query_grad,
        key_grad.reshape(seq_len, col_count).astype(jnp.bfloat16),
        value_grad.reshape(seq_len, col_count).astype(jnp.bfloat16),
    )


def column_sum(values):
    return jnp.sum(values.astype(jnp.float32), axis=0, keepdims=True)


def add_tuples(first, second):
    if first is None:
        return second
    return tuple((left + right for left, right in zip(first, second)))


def pack_grads(gradients, scatter_dims, shard_count):
    pieces = []
    for gradient, scatter_dim in zip(gradients, scatter_dims):
        row_size, col_size = gradient.shape
        if scatter_dim == 0:
            pieces.append(gradient.reshape(shard_count, row_size // shard_count * col_size))
        else:
            moved = gradient.reshape(row_size, shard_count, col_size // shard_count).transpose(
                1, 0, 2
            )
            pieces.append(moved.reshape(shard_count, row_size * (col_size // shard_count)))
    return jnp.concatenate(pieces, axis=1)


def unpack_grads(flattened, gradients, scatter_dims, shard_count):
    results = []
    offset = 0
    for gradient, scatter_dim in zip(gradients, scatter_dims):
        row_size, col_size = gradient.shape
        if scatter_dim == 0:
            target = (row_size // shard_count, col_size)
        else:
            target = (row_size, col_size // shard_count)
        length = target[0] * target[1]
        results.append(flattened[0, offset : offset + length].reshape(target))
        offset = offset + length
    return tuple(results)


def shards(
    inputs,
    w_query,
    w_key,
    w_value,
    b_query,
    b_value,
    w_output,
    b_output,
    attn_gain,
    attn_shift,
    w_up,
    b_up,
    w_down,
    b_down,
    mlp_gain,
    mlp_shift,
    doc_lengths,
    out_grad,
):
    vector_rows = lax.all_gather(
        jnp.stack([b_output, attn_gain, attn_shift, b_down, mlp_gain, mlp_shift]),
        ("fsdp", "tp"),
        axis=1,
        tiled=True,
    ).astype(jnp.float32)
    out_bias = vector_rows[0]
    gain_one = vector_rows[1]
    shift_one = vector_rows[2]
    down_bias = vector_rows[3]
    gain_two = vector_rows[4]
    shift_two = vector_rows[5]
    shard_count = lax.axis_size("fsdp")
    grad_dims = (0, 0, 0, 1, 0, 1, 1, 1, 1)
    weight_sums = None
    shard_sums = None
    vector_sums = jnp.zeros(vector_rows.shape, jnp.float32)
    row_outs = []
    row_grads = []
    for batch_index in range(inputs.shape[0]):
        (
            query_full,
            key_full,
            value_full,
            output_full,
            up_full,
            down_full,
            query_bias,
            value_bias,
            up_bias,
        ) = (
            lax.all_gather(w_query, "fsdp", axis=0, tiled=True),
            lax.all_gather(w_key, "fsdp", axis=0, tiled=True),
            lax.all_gather(w_value, "fsdp", axis=0, tiled=True),
            lax.all_gather(w_output, "fsdp", axis=1, tiled=True),
            lax.all_gather(w_up, "fsdp", axis=0, tiled=True),
            lax.all_gather(w_down, "fsdp", axis=1, tiled=True),
            lax.all_gather(b_query, "fsdp", axis=1, tiled=True),
            lax.all_gather(b_value, "fsdp", axis=1, tiled=True),
            lax.all_gather(b_up, "fsdp", axis=1, tiled=True),
        )
        token_rows = inputs[batch_index]
        gathered = lax.all_gather(token_rows, "tp", axis=0, tiled=True)
        segments, places = segment_ids(doc_lengths[batch_index, 0], gathered.shape[0])
        query_rows = (
            jnp.dot(gathered, query_full, preferred_element_type=jnp.float32)
            + query_bias.astype(jnp.float32)
        ).astype(jnp.bfloat16)
        key_rows = jnp.dot(gathered, key_full, preferred_element_type=jnp.float32).astype(
            jnp.bfloat16
        )
        value_rows = (
            jnp.dot(gathered, value_full, preferred_element_type=jnp.float32)
            + value_bias.astype(jnp.float32)
        ).astype(jnp.bfloat16)
        context, logsums = attention_forward(query_rows, key_rows, value_rows, segments, places)
        attn_part = jnp.dot(context, output_full, preferred_element_type=jnp.float32)
        attn_rows = lax.psum_scatter(
            attn_part.astype(jnp.bfloat16), "tp", scatter_dimension=0, tiled=True
        ).astype(jnp.float32)
        first_out, normed_one, inverse_one = norm_forward(
            token_rows.astype(jnp.float32) + attn_rows + out_bias, gain_one, shift_one
        )
        hidden_rows = first_out.astype(jnp.bfloat16)
        hidden_full = lax.all_gather(hidden_rows, "tp", axis=0, tiled=True)
        up_pre = jnp.dot(hidden_full, up_full, preferred_element_type=jnp.float32) + up_bias.astype(
            jnp.float32
        )
        activated = jax.nn.gelu(up_pre, approximate=True).astype(jnp.bfloat16)
        mlp_rows = lax.psum_scatter(
            jnp.dot(activated, down_full, preferred_element_type=jnp.float32).astype(jnp.bfloat16),
            "tp",
            scatter_dimension=0,
            tiled=True,
        ).astype(jnp.float32)
        layer_rows, normed_two, inverse_two = norm_forward(
            hidden_rows.astype(jnp.float32) + mlp_rows + down_bias, gain_two, shift_two
        )
        row_outs.append(layer_rows.astype(jnp.bfloat16))
        upstream = out_grad[batch_index].astype(jnp.float32)
        second_grad, gain_two_grad, shift_two_grad = norm_backward(
            upstream, normed_two, inverse_two, gain_two
        )
        mixed_full = lax.all_gather(second_grad.astype(jnp.bfloat16), "tp", axis=0, tiled=True)
        down_grad = jnp.einsum(
            "sf,sd->fd", activated, mixed_full, preferred_element_type=jnp.float32
        )
        act_grad = jnp.einsum(
            "sd,fd->sf", mixed_full, down_full, preferred_element_type=jnp.float32
        )
        up_grad = jax.vjp(partial(jax.nn.gelu, approximate=True), up_pre)[1](act_grad)[0].astype(
            jnp.bfloat16
        )
        up_weight_grad = jnp.einsum(
            "sd,sf->df", hidden_full, up_grad, preferred_element_type=jnp.float32
        )
        back_rows = lax.psum_scatter(
            jnp.einsum("sf,df->sd", up_grad, up_full, preferred_element_type=jnp.float32).astype(
                jnp.bfloat16
            ),
            "tp",
            scatter_dimension=0,
            tiled=True,
        ).astype(jnp.float32)
        first_grad, gain_one_grad, shift_one_grad = norm_backward(
            second_grad + back_rows, normed_one, inverse_one, gain_one
        )
        attn_full = lax.all_gather(first_grad.astype(jnp.bfloat16), "tp", axis=0, tiled=True)
        output_grad = jnp.einsum(
            "sc,sd->cd", context, attn_full, preferred_element_type=jnp.float32
        )
        context_grad = jnp.einsum(
            "sd,cd->sc", attn_full, output_full, preferred_element_type=jnp.float32
        ).astype(jnp.bfloat16)
        query_grad, key_grad, value_grad = attention_backward(
            query_rows, key_rows, value_rows, context_grad, logsums, segments, places
        )
        query_weight_grad = jnp.einsum(
            "sd,sc->dc", gathered, query_grad, preferred_element_type=jnp.float32
        )
        key_weight_grad = jnp.einsum(
            "sd,sc->dc", gathered, key_grad, preferred_element_type=jnp.float32
        )
        value_weight_grad = jnp.einsum(
            "sd,sc->dc", gathered, value_grad, preferred_element_type=jnp.float32
        )
        token_part = (
            jnp.einsum("sc,dc->sd", query_grad, query_full, preferred_element_type=jnp.float32)
            + jnp.einsum("sc,dc->sd", key_grad, key_full, preferred_element_type=jnp.float32)
            + jnp.einsum("sc,dc->sd", value_grad, value_full, preferred_element_type=jnp.float32)
        )
        token_back = lax.psum_scatter(
            token_part.astype(jnp.bfloat16), "tp", scatter_dimension=0, tiled=True
        ).astype(jnp.float32)
        row_grads.append((first_grad + token_back).astype(jnp.bfloat16))
        vector_sums = vector_sums + jnp.stack(
            [
                jnp.sum(first_grad, axis=0),
                gain_one_grad,
                shift_one_grad,
                jnp.sum(second_grad, axis=0),
                gain_two_grad,
                shift_two_grad,
            ]
        )
        batch_grads = (
            query_weight_grad,
            key_weight_grad,
            value_weight_grad,
            output_grad,
            up_weight_grad,
            down_grad,
            column_sum(query_grad),
            column_sum(value_grad),
            column_sum(up_grad),
        )
        weight_sums = add_tuples(weight_sums, batch_grads)
    packed = pack_grads(weight_sums, grad_dims, shard_count)
    summed = lax.psum_scatter(
        packed.astype(jnp.bfloat16), "fsdp", scatter_dimension=0, tiled=True
    ).astype(jnp.float32)
    shard_sums = unpack_grads(summed, weight_sums, grad_dims, shard_count)
    vector_shards = lax.psum_scatter(vector_sums, ("fsdp", "tp"), scatter_dimension=1, tiled=True)
    return (
        jnp.stack(row_outs),
        jnp.stack(row_grads),
        shard_sums[0],
        shard_sums[1],
        shard_sums[2],
        shard_sums[6],
        shard_sums[7],
        shard_sums[3],
        vector_shards[0],
        vector_shards[1],
        vector_shards[2],
        shard_sums[4],
        shard_sums[8],
        shard_sums[5],
        vector_shards[3],
        vector_shards[4],
        vector_shards[5],
    )


AXES = ("fsdp", "tp")
TN = (((0,), (0,)), ((), ()))
NT = (((1,), (1,)), ((), ()))
VMEM_LIMIT = 60 * 1024 * 1024
ANY = pl.BlockSpec(memory_space=pl.ANY)
STEPS = (0, 2, 1, 3)


def params(**kwargs):
    return pltpu.CompilerParams(vmem_limit_bytes=VMEM_LIMIT, **kwargs)


def dot(left, right, dims=(((1,), (0,)), ((), ()))):
    return lax.dot_general(left, right, dims, preferred_element_type=jnp.float32)


def place_of(step):
    return (step % 2) * 2 + step // 2


def swap(values, fsdp_bits, tp_bits):
    fsdp_size, tp_size = lax.axis_size("fsdp"), lax.axis_size("tp")
    pairs = [
        (f * tp_size + t, (f ^ fsdp_bits) * tp_size + (t ^ tp_bits))
        for f in range(fsdp_size)
        for t in range(tp_size)
    ]
    return lax.ppermute(values, AXES, pairs)


def home_pairs(second):
    pairs = []
    for group in range(lax.axis_size("fsdp") // 2):
        for core in range(2):
            for t in range(4):
                micro = (t % 2) ^ second
                pairs.append(((group * 2 + core) * 4 + t, (group * 2 + t // 2) * 4 + micro * 2 + core))
    return pairs


def to_sequences(rows, t):
    odd = t % 2
    first = lax.dynamic_index_in_dim(rows, odd, 0, keepdims=False)
    second = lax.dynamic_index_in_dim(rows, 1 - odd, 0, keepdims=False)
    return (lax.ppermute(first, AXES, home_pairs(0)), lax.ppermute(second, AXES, home_pairs(1)))


def to_homes(rows, t):
    micro = t // 2
    halves = rows.reshape(2, rows.shape[0] // 2, rows.shape[1])
    first = lax.dynamic_index_in_dim(halves, micro, 0, keepdims=False)
    second = lax.dynamic_index_in_dim(halves, 1 - micro, 0, keepdims=False)
    first = lax.ppermute(first, AXES, [(b, a) for a, b in home_pairs(0)])
    second = lax.ppermute(second, AXES, [(b, a) for a, b in home_pairs(1)])
    odd = t % 2
    return jnp.where(odd == 0, jnp.stack([first, second]), jnp.stack([second, first]))


def gather_pieces(shard, first_bits, second_bits):
    pair = jnp.stack([shard, swap(shard, 0, 2)])
    quad = jnp.concatenate([pair, swap(pair, 0, 1)])
    pieces = {0: quad}
    pieces[first_bits] = swap(quad, first_bits, 0)
    pieces[second_bits] = swap(quad, second_bits, 0)
    pieces[6] = swap(pieces[first_bits], second_bits, 0)
    for offset in (0, first_bits, second_bits, 6):
        pieces[offset + 1] = swap(pieces[offset], 1, 0)
    return [pieces[offset] for offset in range(8)]


def qkv_kernel(info, *refs):
    pieces, tokens, biases = refs[:8], refs[8:12], refs[12]
    rows_ref, weight_ref, query_ref, key_ref, value_ref = refs[13:18]
    row_sems, weight_sems = refs[18:]
    f, t, core, micro = info[0], info[1], info[2], info[3]
    copies = []
    for offset in range(8):
        block = f ^ offset
        for j in range(2):
            place = place_of(t ^ (2 * core + j))
            for which in range(3):
                copies.append(
                    pltpu.make_async_copy(
                        pieces[offset].at[place, pl.ds(which * 128, 128), :],
                        weight_ref.at[which, pl.ds(pl.multiple_of(block * 128, 128), 128), pl.ds(j * 256, 256)],
                        weight_sems.at[len(copies)],
                    )
                )
    for k in range(4):
        quarter = (k // 2) * 2 + (micro if k % 2 == 0 else 1 - micro)
        copies.append(
            pltpu.make_async_copy(
                tokens[k], rows_ref.at[pl.ds(pl.multiple_of(quarter * 512, 512), 512), :], row_sems.at[k]
            )
        )
    for copy in copies:
        copy.start()
    for copy in copies:
        copy.wait()
    for block in range(8):
        span = pl.ds(block * 256, 256)
        rows = rows_ref[span, :]
        query_ref[span, :] = (
            (dot(rows, weight_ref[0]) + biases[0:1, :]).astype(jnp.bfloat16).astype(jnp.float32)
            * HEAD_DIM ** (-0.5)
        ).astype(jnp.bfloat16)
        key_ref[span, :] = dot(rows, weight_ref[1]).astype(jnp.bfloat16)
        value_ref[span, :] = (dot(rows, weight_ref[2]) + biases[1:2, :]).astype(jnp.bfloat16)


def project(info, pieces, tokens, biases):
    head_rows = jax.ShapeDtypeStruct((2048, 512), jnp.bfloat16)
    whole = pl.BlockSpec(memory_space=pltpu.VMEM)
    return pl.pallas_call(
        qkv_kernel,
        out_shape=(
            jax.ShapeDtypeStruct((2048, 1024), jnp.bfloat16),
            jax.ShapeDtypeStruct((3, 1024, 512), jnp.bfloat16),
            head_rows,
            head_rows,
            head_rows,
        ),
        grid_spec=pltpu.PrefetchScalarGridSpec(
            num_scalar_prefetch=1,
            grid=(),
            in_specs=[ANY] * 12 + [whole],
            out_specs=[whole] * 5,
            scratch_shapes=[pltpu.SemaphoreType.DMA((4,)), pltpu.SemaphoreType.DMA((48,))],
        ),
        compiler_params=params(),
        name="qkv",
    )(info, *pieces, *tokens, biases)


def head_mask(rows):
    return lax.broadcasted_iota(jnp.int32, (rows, 128), 1) < HEAD_DIM


def split_heads(pair):
    low = head_mask(pair.shape[0])
    zero = jnp.zeros_like(pair)
    return (jnp.where(low, pair, zero), jnp.where(low, zero, pair))


def three_loops(info, block, body, carry):
    base = 8 + block * 4
    lo, hi, full_lo, full_hi = info[base], info[base + 1], info[base + 2], info[base + 3]
    carry = lax.fori_loop(lo, full_lo, partial(body, True), carry)
    carry = lax.fori_loop(full_lo, full_hi, partial(body, False), carry)
    return lax.fori_loop(full_hi, hi, partial(body, True), carry)


def key_span(info, block):
    return pl.ds(pl.multiple_of((block ^ (info[2] * 4)) * 256, 256), 256)


def masked(scores, bounds_ref, block):
    places = block * 256 + lax.broadcasted_iota(jnp.int32, scores.shape, 0)
    allowed = (places >= bounds_ref[0:1, :]) & (places < bounds_ref[1:2, :])
    return jnp.where(allowed, scores, MASKED)


def attend_kernel(first_block, info, query_ref, key_ref, value_ref, bounds_ref, context_ref, lse_ref, turned):
    step = pl.program_id(1)

    @pl.when(step == 0)
    def _():
        turned[...] = value_ref[...].T

    queries = split_heads(query_ref[...])

    def body(use_mask, block, carry):
        span = key_span(info, block)
        keys = key_ref[span, :]
        out = []
        for h in range(2):
            top, total, context = carry[h]
            scores = dot(keys, queries[h], NT)
            if use_mask:
                scores = masked(scores, bounds_ref, block)
            new_top = jnp.maximum(top, jnp.max(scores, axis=0, keepdims=True))
            decay = jnp.exp(top - new_top)
            exponent = jnp.exp(scores - new_top)
            total = total * decay + jnp.sum(exponent, axis=0, keepdims=True)
            context = context * decay + dot(
                turned[h * HEAD_DIM : (h + 1) * HEAD_DIM, span], exponent.astype(jnp.bfloat16)
            )
            out.append((new_top, total, context))
        return tuple(out)

    start = (
        jnp.full((1, 256), 2 * MASKED, jnp.float32),
        jnp.zeros((1, 256), jnp.float32),
        jnp.zeros((HEAD_DIM, 256), jnp.float32),
    )
    heads = three_loops(info, first_block + step, body, (start, start))
    context_ref[...] = jnp.concatenate(
        [context / total for _, total, context in heads], axis=0
    ).T.astype(jnp.bfloat16)
    lse_ref[0, 0:1, :] = heads[0][0] + jnp.log(heads[0][1])
    lse_ref[0, 1:2, :] = heads[1][0] + jnp.log(heads[1][1])


def attend(info, queries, keys, values, bounds, half):
    first_block = half * 4
    return pl.pallas_call(
        partial(attend_kernel, first_block),
        out_shape=(
            jax.ShapeDtypeStruct((1024, 512), jnp.bfloat16),
            jax.ShapeDtypeStruct((4, 8, 1024), jnp.float32),
        ),
        grid_spec=pltpu.PrefetchScalarGridSpec(
            num_scalar_prefetch=1,
            grid=(4, 4),
            in_specs=[
                pl.BlockSpec((256, 128), lambda p, i, s: (first_block + i, p)),
                pl.BlockSpec((2048, 128), lambda p, i, s: (0, p)),
                pl.BlockSpec((2048, 128), lambda p, i, s: (0, p)),
                pl.BlockSpec((8, 256), lambda p, i, s: (0, first_block + i)),
            ],
            out_specs=[
                pl.BlockSpec((256, 128), lambda p, i, s: (i, p)),
                pl.BlockSpec((1, 8, 256), lambda p, i, s: (p, 0, i)),
            ],
            scratch_shapes=[pltpu.VMEM((128, 2048), jnp.bfloat16)],
        ),
        compiler_params=params(),
        name="attend",
    )(info, queries, keys, values, bounds)


def attend_back_kernel(
    info, query_ref, key_ref, value_ref, bounds_ref,
    context_own, context_other, grad_own, grad_other, lse_own, lse_other,
    query_grad, key_grad, value_grad, query_sum, value_sum,
    turned, key_total, value_total,
):
    step = pl.program_id(1)

    @pl.when(step == 0)
    def _():
        turned[...] = key_ref[...].T
        key_total[...] = jnp.zeros_like(key_total)
        value_total[...] = jnp.zeros_like(value_total)
        query_sum[...] = jnp.zeros_like(query_sum)

    own = step < 4
    context = jnp.where(own, context_own[...], context_other[...])
    grad_pair = jnp.where(own, grad_own[...], grad_other[...])
    lse = jnp.where(own, lse_own[0], lse_other[0])
    product = (context.astype(jnp.float32) * grad_pair.astype(jnp.float32)).T
    queries = split_heads(query_ref[...])
    grads = split_heads(grad_pair)
    query_stack = jnp.concatenate(queries, axis=0)
    grad_stack = jnp.concatenate(grads, axis=0)
    deltas = [
        jnp.sum(product[h * HEAD_DIM : (h + 1) * HEAD_DIM], axis=0, keepdims=True) for h in range(2)
    ]

    def body(use_mask, block, carry):
        span = key_span(info, block)
        keys = key_ref[span, :]
        values = value_ref[span, :]
        probs, slopes, out = [], [], []
        for h in range(2):
            scores = dot(keys, queries[h], NT)
            if use_mask:
                scores = masked(scores, bounds_ref, block)
            prob = jnp.exp(scores - lse[h : h + 1, :])
            prob_grad = dot(values, grads[h], NT)
            slope = (prob * (prob_grad - deltas[h])).astype(jnp.bfloat16)
            probs.append(prob.astype(jnp.bfloat16))
            slopes.append(slope)
            out.append(carry[h] + dot(turned[h * HEAD_DIM : (h + 1) * HEAD_DIM, span], slope))
        value_total[span, :] += dot(jnp.concatenate(probs, axis=1), grad_stack)
        key_total[span, :] += dot(jnp.concatenate(slopes, axis=1), query_stack)
        return tuple(out)

    zero = jnp.zeros((HEAD_DIM, 256), jnp.float32)
    heads = three_loops(info, step, body, (zero, zero))
    rows = (jnp.concatenate(heads, axis=0).T * HEAD_DIM ** (-0.5)).astype(jnp.bfloat16)
    query_grad[...] = rows
    query_sum[0:1, :] += jnp.sum(rows.astype(jnp.float32), axis=0, keepdims=True)

    @pl.when(step == pl.num_programs(1) - 1)
    def _():
        key_grad[...] = key_total[...].astype(jnp.bfloat16)
        rounded = value_total[...].astype(jnp.bfloat16)
        value_grad[...] = rounded
        value_sum[...] = jnp.zeros_like(value_sum)
        value_sum[0:1, :] = jnp.sum(rounded.astype(jnp.float32), axis=0, keepdims=True)


def attend_back(info, queries, keys, values, bounds, contexts, grads, lses):
    rows = jax.ShapeDtypeStruct((2048, 512), jnp.bfloat16)
    sums = jax.ShapeDtypeStruct((8, 512), jnp.float32)
    own = pl.BlockSpec((256, 128), lambda p, i, s: (jnp.minimum(i, 3), p))
    other = pl.BlockSpec((256, 128), lambda p, i, s: (jnp.maximum(i - 4, 0), p))
    column = pl.BlockSpec((2048, 128), lambda p, i, s: (0, p))
    sum_spec = pl.BlockSpec((8, 128), lambda p, i, s: (0, p))
    return pl.pallas_call(
        attend_back_kernel,
        out_shape=(rows, rows, rows, sums, sums),
        grid_spec=pltpu.PrefetchScalarGridSpec(
            num_scalar_prefetch=1,
            grid=(4, 8),
            in_specs=[
                pl.BlockSpec((256, 128), lambda p, i, s: (i, p)),
                column,
                column,
                pl.BlockSpec((8, 256), lambda p, i, s: (0, i)),
                own,
                other,
                own,
                other,
                pl.BlockSpec((1, 8, 256), lambda p, i, s: (p, 0, jnp.minimum(i, 3))),
                pl.BlockSpec((1, 8, 256), lambda p, i, s: (p, 0, jnp.maximum(i - 4, 0))),
            ],
            out_specs=[
                pl.BlockSpec((256, 128), lambda p, i, s: (i, p)),
                column,
                column,
                sum_spec,
                sum_spec,
            ],
            scratch_shapes=[
                pltpu.VMEM((128, 2048), jnp.bfloat16),
                pltpu.VMEM((2048, 128), jnp.float32),
                pltpu.VMEM((2048, 128), jnp.float32),
            ],
        ),
        compiler_params=params(),
        name="attend_back",
    )(info, queries, keys, values, bounds, *contexts, *grads, *lses)


def normed(values):
    average = jnp.mean(values, axis=-1, keepdims=True)
    centred = values - average
    inverse = lax.rsqrt(jnp.mean(centred * centred, axis=-1, keepdims=True) + EPSILON)
    return (centred * inverse, inverse)


def normed_back(upstream, unit, inverse, gain):
    scaled = upstream * gain
    inner_mean = jnp.mean(scaled, axis=-1, keepdims=True)
    cross_mean = jnp.mean(scaled * unit, axis=-1, keepdims=True)
    return inverse * (scaled - inner_mean - unit * cross_mean)


def column_total(values):
    return jnp.sum(values, axis=0, keepdims=True)


def middle_kernel(info, *refs):
    up_pieces, down_pieces = refs[:8], refs[8:16]
    own_ref, other_ref, token_ref, upstream_ref, vector_ref, up_bias_ref = refs[16:22]
    (
        layer_ref, hidden_ref, act_ref, mixed_ref, up_grad_ref, attended_ref, first_ref,
        grad_own_ref, grad_other_ref, sums_ref, up_sum_ref,
    ) = refs[22:33]
    up_weight, down_weight, out_weight, slope_ref, sems = refs[33:]
    f, t, core = info[0], info[1], info[2]
    step = pl.program_id(0)

    @pl.when(step == 0)
    def _():
        out_copies, up_copies, down_copies = [], [], []
        for offset in range(8):
            columns = pl.ds(pl.multiple_of((f ^ offset) * 128, 128), 128)
            for place in range(4):
                slice_of = t ^ STEPS[place]
                row = ((slice_of // 2) ^ core) * 512 + (slice_of % 2) * 256
                out_copies.append(
                    pltpu.make_async_copy(
                        down_pieces[offset].at[place, pl.ds(1024, 256), :],
                        out_weight.at[pl.ds(pl.multiple_of(row, 256), 256), columns],
                        sems.at[16 + offset * 4 + place],
                    )
                )
            up_copies.append(
                pltpu.make_async_copy(up_pieces[offset], up_weight.at[:, columns, :], sems.at[offset])
            )
            down_copies.append(
                pltpu.make_async_copy(
                    down_pieces[offset].at[:, pl.ds(0, 1024), :],
                    down_weight.at[:, :, columns],
                    sems.at[8 + offset],
                )
            )
        copies = out_copies + up_copies + down_copies
        for copy in copies:
            copy.start()
        for copy in copies:
            copy.wait()
        sums_ref[...] = jnp.zeros_like(sums_ref)
        up_sum_ref[...] = jnp.zeros_like(up_sum_ref)

    vectors = [vector_ref[k : k + 1, :] for k in range(6)]
    out_bias, gain_one, shift_one, down_bias, gain_two, shift_two = vectors
    attended = dot(own_ref[...], out_weight[0:512, :]) + dot(other_ref[...], out_weight[512:1024, :])
    unit_one, inverse_one = normed(token_ref[...].astype(jnp.float32) + attended + out_bias)
    hidden = (unit_one * gain_one + shift_one).astype(jnp.bfloat16)
    hidden_ref[...] = hidden
    mixed = jnp.zeros(unit_one.shape, jnp.float32)
    for place in range(4):
        span = pl.ds(place * 1024, 1024)
        pre = dot(hidden, up_weight[place]) + up_bias_ref[place : place + 1, :]
        square = pre * pre
        bend = jnp.tanh(0.7978845608028654 * pre * (1.0 + 0.044715 * square))
        half = 0.5 * (1.0 + bend)
        act = (pre * half).astype(jnp.bfloat16)
        act_ref[:, span] = act
        slope_ref[:, span] = half + 0.5 * pre * (1.0 - bend * bend) * (
            0.7978845608028654 * (1.0 + 0.134145 * square)
        )
        mixed = mixed + dot(act, down_weight[place])
    unit_two, inverse_two = normed(hidden.astype(jnp.float32) + mixed + down_bias)
    layer_ref[...] = (unit_two * gain_two + shift_two).astype(jnp.bfloat16)
    upstream = upstream_ref[...].astype(jnp.float32)
    second = normed_back(upstream, unit_two, inverse_two, gain_two)
    sums_ref[3:4, :] += column_total(second)
    sums_ref[4:5, :] += column_total(upstream * unit_two)
    sums_ref[5:6, :] += column_total(upstream)
    mixed_grad = second.astype(jnp.bfloat16)
    mixed_ref[...] = mixed_grad
    back = second
    for place in range(4):
        span = pl.ds(place * 1024, 1024)
        up_grad = (dot(mixed_grad, down_weight[place], NT) * slope_ref[:, span]).astype(jnp.bfloat16)
        up_grad_ref[:, span] = up_grad
        up_sum_ref[place : place + 1, :] += column_total(up_grad.astype(jnp.float32))
        back = back + dot(up_grad, up_weight[place], NT)
    first = normed_back(back, unit_one, inverse_one, gain_one)
    sums_ref[0:1, :] += column_total(first)
    sums_ref[1:2, :] += column_total(back * unit_one)
    sums_ref[2:3, :] += column_total(back)
    first_ref[...] = first
    rounded = first.astype(jnp.bfloat16)
    attended_ref[...] = rounded
    grad_own_ref[...] = dot(rounded, out_weight[0:512, :], NT).astype(jnp.bfloat16)
    grad_other_ref[...] = dot(rounded, out_weight[512:1024, :], NT).astype(jnp.bfloat16)


def middle(info, up_pieces, down_pieces, own, other, tokens, upstream, vectors, up_bias):
    tile = 256

    def rows(width):
        return pl.BlockSpec((tile, width), lambda i, s: (i, 0))

    def fixed(shape):
        return pl.BlockSpec(shape, lambda i, s: (0, 0))

    def array(width, kind=jnp.bfloat16):
        return jax.ShapeDtypeStruct((1024, width), kind)

    return pl.pallas_call(
        middle_kernel,
        out_shape=(
            array(1024), array(1024), array(4096), array(1024), array(4096), array(1024),
            array(1024, jnp.float32), array(512), array(512),
            jax.ShapeDtypeStruct((8, 1024), jnp.float32),
            jax.ShapeDtypeStruct((8, 1024), jnp.float32),
        ),
        grid_spec=pltpu.PrefetchScalarGridSpec(
            num_scalar_prefetch=1,
            grid=(4,),
            in_specs=[ANY] * 16
            + [rows(512), rows(512), rows(1024), rows(1024), fixed((8, 1024)), fixed((8, 1024))],
            out_specs=[
                rows(1024), rows(1024), rows(4096), rows(1024), rows(4096), rows(1024),
                rows(1024), rows(512), rows(512), fixed((8, 1024)), fixed((8, 1024)),
            ],
            scratch_shapes=[
                pltpu.VMEM((4, 1024, 1024), jnp.bfloat16),
                pltpu.VMEM((4, 1024, 1024), jnp.bfloat16),
                pltpu.VMEM((1024, 1024), jnp.bfloat16),
                pltpu.VMEM((tile, 4096), jnp.float32),
                pltpu.SemaphoreType.DMA((48,)),
            ],
        ),
        compiler_params=params(),
        name="middle",
    )(info, *up_pieces, *down_pieces, own, other, tokens, upstream, vectors, up_bias)


def turn_columns(turned, refs):
    for k in range(4):
        turned[k * 128 : (k + 1) * 128, :] = refs[k][...].T


def wide_grad_kernel(has_other, info, *refs):
    left, right = refs[:4], refs[4]
    others = refs[5:7] if has_other else None
    keep_ref, send_ref, turned = refs[-3:]

    @pl.when(pl.program_id(0) == 0)
    def _():
        turn_columns(turned, left)

    result = dot(turned[...], right[...])
    for k in range(4):
        part = result[k * 128 : (k + 1) * 128]
        target = keep_ref if k < 2 else send_ref
        if has_other:
            part = part + others[k // 2][k % 2, 0].astype(jnp.float32)
        target[k % 2, 0] = part.astype(jnp.bfloat16)


def left_specs(rows, order, core_bit):
    return [
        pl.BlockSpec((rows, 128), lambda n, s, o=offset: (0, s[0] ^ (o | core_bit))) for offset in order
    ]


def wide_grad(info, left, right, order, core_bit, others=None):
    shape = jax.ShapeDtypeStruct((2, 4, 128, 1024), jnp.bfloat16)
    part = pl.BlockSpec((2, 1, 128, 512), lambda n, s: (0, n // 2, 0, n % 2))
    return pl.pallas_call(
        partial(wide_grad_kernel, others is not None),
        out_shape=(shape, shape),
        grid_spec=pltpu.PrefetchScalarGridSpec(
            num_scalar_prefetch=1,
            grid=(8,),
            in_specs=left_specs(1024, order, core_bit)
            + [pl.BlockSpec((1024, 512), lambda n, s: (0, n))]
            + ([part, part] if others is not None else []),
            out_specs=[part, part],
            scratch_shapes=[pltpu.VMEM((512, 1024), jnp.bfloat16)],
        ),
        compiler_params=params(),
        name="wide_grad",
    )(info, left, left, left, left, right, *(others or ()))


def out_grad_kernel(has_other, info, *refs):
    left, own, other = refs[:4], refs[4], refs[5]
    others = refs[6:8] if has_other else None
    keep_ref, send_ref, turned = refs[-3:]
    step = pl.program_id(0)

    @pl.when(step == 0)
    def _():
        turn_columns(turned, left)

    result = dot(turned[...], jnp.where(step < 2, own[...], other[...]))
    for k in range(4):
        part = result[k * 128 : (k + 1) * 128]
        target = keep_ref if k < 2 else send_ref
        if has_other:
            part = part + others[k // 2][k % 2, 0].astype(jnp.float32)
        target[k % 2, 0] = part.astype(jnp.bfloat16)


def out_grad_parts(info, left, own, other, order, core_bit, others=None):
    shape = jax.ShapeDtypeStruct((2, 4, 128, 256), jnp.bfloat16)

    def place(n, s):
        return place_of(s[1] ^ (2 * ((n // 2) ^ s[2]) + n % 2))

    part = pl.BlockSpec((2, 1, 128, 256), lambda n, s: (0, place(n, s), 0, 0))
    return pl.pallas_call(
        partial(out_grad_kernel, others is not None),
        out_shape=(shape, shape),
        grid_spec=pltpu.PrefetchScalarGridSpec(
            num_scalar_prefetch=1,
            grid=(4,),
            in_specs=left_specs(1024, order, core_bit)
            + [
                pl.BlockSpec((1024, 256), lambda n, s: (0, jnp.minimum(n, 1))),
                pl.BlockSpec((1024, 256), lambda n, s: (0, jnp.maximum(n - 2, 0))),
            ]
            + ([part, part] if others is not None else []),
            out_specs=[part, part],
            scratch_shapes=[pltpu.VMEM((512, 1024), jnp.bfloat16)],
        ),
        compiler_params=params(),
        name="out_grad",
    )(info, left, left, left, left, own, other, *(others or ()))


def qkv_grad_kernel(info, *refs):
    left, rights = refs[:4], refs[4:7]
    keep_ref, send_ref, turned = refs[-3:]

    @pl.when(pl.program_id(0) == 0)
    def _():
        turn_columns(turned, left)

    for which in range(3):
        result = dot(turned[...], rights[which][...])
        for k in range(4):
            target = keep_ref if k < 2 else send_ref
            target[k % 2, 0, which] = result[k * 128 : (k + 1) * 128].astype(jnp.bfloat16)


def qkv_grad(info, left, rights, order, core_bit):
    shape = jax.ShapeDtypeStruct((2, 2, 3, 128, 256), jnp.bfloat16)
    part = pl.BlockSpec((2, 1, 3, 128, 256), lambda n, s: (0, n, 0, 0, 0))
    return pl.pallas_call(
        qkv_grad_kernel,
        out_shape=(shape, shape),
        grid_spec=pltpu.PrefetchScalarGridSpec(
            num_scalar_prefetch=1,
            grid=(2,),
            in_specs=left_specs(2048, order, core_bit)
            + [pl.BlockSpec((2048, 256), lambda n, s: (0, n))] * 3,
            out_specs=[part, part],
            scratch_shapes=[pltpu.VMEM((512, 2048), jnp.bfloat16)],
        ),
        compiler_params=params(),
        name="qkv_grad",
    )(info, left, left, left, left, *rights)


def token_grad_kernel(has_other, info, *refs):
    grads, weight = refs[:3], refs[3]
    total = dot(grads[0][...], weight[0], NT)
    total = total + dot(grads[1][...], weight[1], NT)
    total = total + dot(grads[2][...], weight[2], NT)
    if has_other:
        total = total + refs[4][...].astype(jnp.float32) + refs[5][...]
    refs[-1][...] = total.astype(jnp.bfloat16)


def token_grad(info, grads, weight, half, other=None, first=None):
    extra = [] if other is None else [other, first]
    return pl.pallas_call(
        partial(token_grad_kernel, other is not None),
        out_shape=jax.ShapeDtypeStruct((1024, 1024), jnp.bfloat16),
        grid_spec=pltpu.PrefetchScalarGridSpec(
            num_scalar_prefetch=1,
            grid=(4,),
            in_specs=[pl.BlockSpec((256, 512), lambda i, s: (half * 4 + i, 0))] * 3
            + [pl.BlockSpec((3, 1024, 512), lambda i, s: (0, 0, 0))]
            + [pl.BlockSpec((256, 1024), lambda i, s: (i, 0))] * len(extra),
            out_specs=pl.BlockSpec((256, 1024), lambda i, s: (i, 0)),
        ),
        compiler_params=params(),
        name="token_grad",
    )(info, *grads, weight, *extra)


def low(values):
    return values.astype(jnp.bfloat16)


def wide(values):
    return values.astype(jnp.float32)


def plane_sums(keep, send, first_bits, second_bits):
    came = swap(send, first_bits, 0)
    passed = swap(low(wide(keep[1]) + wide(came[1])), second_bits, 0)
    return wide(keep[0]) + wide(came[0]) + wide(passed)


def column_sums(total):
    came = swap(low(total[2:4]), 0, 1)
    total = total[0:2] + wide(came)
    return total[0] + wide(swap(low(total[1]), 0, 2))


def chip_shards(
    inputs,
    w_query,
    w_key,
    w_value,
    b_query,
    b_value,
    w_output,
    b_output,
    attn_gain,
    attn_shift,
    w_up,
    b_up,
    w_down,
    b_down,
    mlp_gain,
    mlp_shift,
    doc_lengths,
    out_grad,
):
    f, t = lax.axis_index("fsdp"), lax.axis_index("tp")
    core, micro = f % 2, t // 2

    narrow = jnp.concatenate(
        [
            jnp.concatenate([b_up[0], b_query[0], b_value[0], jnp.zeros((64,), jnp.bfloat16)])[None],
            jnp.concatenate(
                [b_output, attn_gain, attn_shift, b_down, mlp_gain, mlp_shift, jnp.zeros((64,), jnp.bfloat16)]
            )[None],
            jnp.zeros((14, 256), jnp.bfloat16),
        ]
    )
    qkv_pieces = gather_pieces(jnp.concatenate([w_query, w_key, w_value, narrow]), 2, 4)
    token_a, token_b = to_sequences(inputs, t)
    up_pieces = gather_pieces(w_up, 2, 4)
    down_pieces = gather_pieces(jnp.concatenate([w_down, w_output]), 4, 2)
    upstream_a, upstream_b = to_sequences(out_grad, t)
    other_a, other_b = swap(token_a, 1, 0), swap(token_b, 1, 0)
    lengths = jnp.where(t % 2 == core, doc_lengths, swap(doc_lengths, 1, 0))[micro, 0]

    narrow_rows = jnp.stack([piece[:, 384:386] for piece in qkv_pieces]).reshape(32, 2, 256)
    f_ids, t_ids = jnp.arange(8), jnp.arange(4)
    order = ((f_ids ^ f)[:, None] * 4 + place_of(t_ids ^ t)[None, :]).reshape(-1)
    narrow_rows = wide(jnp.take(narrow_rows, order, axis=0)).reshape(8, 4, 2, 256)
    vectors = narrow_rows[:, :, 1, :192].reshape(32, 6, 32).transpose(1, 0, 2).reshape(6, 1024)
    vectors = jnp.pad(vectors, ((0, 2), (0, 0)))
    quad = t ^ jnp.array(STEPS)
    up_bias = narrow_rows[:, :, 0, :128].transpose(1, 0, 2).reshape(4, 1024)
    up_bias = jnp.pad(jnp.take(up_bias, quad, axis=0), ((0, 4), (0, 0)))
    head_bias = narrow_rows[:, :, 0, 128:192].reshape(8, 4, 2, 32).transpose(2, 1, 0, 3).reshape(2, 2, 512)
    head_bias = lax.dynamic_index_in_dim(head_bias, core, 1, keepdims=False)
    head_bias = jnp.pad(head_bias, ((0, 6), (0, 0)))

    ends = jnp.cumsum(lengths)
    places = jnp.arange(2048, dtype=jnp.int32)
    places = places ^ (core * 1024)
    past = ends[None, :] <= places[:, None]
    doc_start = jnp.max(jnp.where(past, ends[None, :], 0), axis=1)
    doc_end = jnp.min(jnp.where(past, 2048, ends[None, :]), axis=1)
    low_bound = jnp.maximum(doc_start, places - (WINDOW - 1))
    high_bound = jnp.minimum(doc_end, places + WINDOW)
    bounds = jnp.concatenate([low_bound[None], high_bound[None], jnp.zeros((6, 2048), jnp.int32)])
    low_blocks, high_blocks = low_bound.reshape(8, 256), high_bound.reshape(8, 256)
    block_lo = jnp.min(low_blocks, axis=1) // 256
    block_hi = (jnp.max(high_blocks, axis=1) + 255) // 256
    full_lo = (jnp.max(low_blocks, axis=1) + 255) // 256
    full_hi = jnp.min(high_blocks, axis=1) // 256
    none = full_lo >= full_hi
    full_lo, full_hi = jnp.where(none, block_hi, full_lo), jnp.where(none, block_hi, full_hi)
    table = jnp.stack([block_lo, block_hi, full_lo, full_hi], axis=1).reshape(-1)
    info = jnp.concatenate(
        [jnp.stack([f, t, core, micro, core * 0, core * 0, core * 0, core * 0]), table]
    ).astype(jnp.int32)

    tokens, weight, queries, keys, values = project(
        info, qkv_pieces, (token_a, token_b, other_a, other_b), head_bias
    )
    context_sent, lse_other = attend(info, queries, keys, values, bounds, 1)
    context_came = swap(context_sent, 1, 0)
    context_own, lse_own = attend(info, queries, keys, values, bounds, 0)
    upstream = jnp.where(
        micro == 0,
        jnp.concatenate([upstream_a, upstream_b]),
        jnp.concatenate([upstream_b, upstream_a]),
    )
    (
        layer_rows, hidden, act, mixed_grad, up_grad, attended, first,
        grad_own, grad_sent, vector_sums, up_sums,
    ) = middle(info, up_pieces, down_pieces, context_own, context_came, tokens, upstream, vectors, up_bias)
    grad_came = swap(grad_sent, 1, 0)
    layer_out = to_homes(layer_rows, t)

    up_order, down_order = (0, 4, 2, 6), (0, 2, 4, 6)
    down_sent = wide_grad(info, mixed_grad, act, down_order, 1)
    up_sent = wide_grad(info, hidden, up_grad, up_order, 1)
    out_sent = out_grad_parts(info, attended, context_own, context_came, down_order, 1)
    down_came = tuple(swap(part, 1, 0) for part in down_sent)
    up_came = tuple(swap(part, 1, 0) for part in up_sent)
    out_came = tuple(swap(part, 1, 0) for part in out_sent)
    down_parts = wide_grad(info, mixed_grad, act, down_order, 0, down_came)
    up_parts = wide_grad(info, hidden, up_grad, up_order, 0, up_came)
    out_parts = out_grad_parts(info, attended, context_own, context_came, down_order, 0, out_came)
    grad_down = column_sums(plane_sums(*down_parts, 4, 2)).T
    grad_up = column_sums(plane_sums(*up_parts, 2, 4))
    grad_output = column_sums(plane_sums(*out_parts, 4, 2)).T

    by_tp = jnp.take(up_sums[:4], place_of(t_ids ^ t), axis=0)
    sums = jnp.concatenate(
        [
            vector_sums[:6].reshape(6, 32, 32).transpose(1, 0, 2).reshape(32, 192),
            by_tp.reshape(4, 8, 128).transpose(1, 0, 2).reshape(32, 128),
        ],
        axis=1,
    )
    sums = lax.psum_scatter(sums, AXES, scatter_dimension=0, tiled=True)[0]

    query_grad, key_grad, value_grad, query_sum, value_sum = attend_back(
        info, queries, keys, values, bounds,
        (context_own, context_sent), (grad_own, grad_came), (lse_own, lse_other),
    )
    grads = (query_grad, key_grad, value_grad)
    token_sent = token_grad(info, grads, weight, 1)
    token_came = swap(token_sent, 1, 0)
    qkv_sent = qkv_grad(info, tokens, grads, up_order, 1)
    qkv_came = tuple(swap(part, 1, 0) for part in qkv_sent)
    token_rows = token_grad(info, grads, weight, 0, token_came, first)
    input_grad = to_homes(token_rows, t)
    qkv_own = plane_sums(*qkv_grad(info, tokens, grads, up_order, 0), 2, 4)
    qkv_other = plane_sums(*qkv_came, 2, 4)
    by_slice = jnp.where(
        core == 0,
        jnp.concatenate([qkv_own, qkv_other]),
        jnp.concatenate([qkv_other, qkv_own]),
    )
    qkv_total = column_sums(jnp.take(by_slice, quad, axis=0))

    head_sums = jnp.stack([query_sum[0], value_sum[0]])
    head_sums = jnp.where(
        core == 0,
        jnp.concatenate([head_sums, jnp.zeros_like(head_sums)], axis=1),
        jnp.concatenate([jnp.zeros_like(head_sums), head_sums], axis=1),
    )
    head_sums = head_sums.reshape(2, 4, 8, 32).transpose(2, 1, 0, 3).reshape(32, 64)
    head_sums = lax.psum_scatter(head_sums, AXES, scatter_dimension=0, tiled=True)[0]
    return (
        layer_out,
        input_grad,
        qkv_total[0],
        qkv_total[1],
        qkv_total[2],
        head_sums[None, :32],
        head_sums[None, 32:],
        grad_output,
        sums[0:32],
        sums[32:64],
        sums[64:96],
        grad_up,
        sums[None, 192:320],
        grad_down,
        sums[96:128],
        sums[128:160],
        sums[160:192],
    )


def solution(mesh):
    in_specs = (
        P(None, ("fsdp", "tp"), None),
        P("fsdp", "tp"),
        P("fsdp", "tp"),
        P("fsdp", "tp"),
        P("tp", "fsdp"),
        P("tp", "fsdp"),
        P("tp", "fsdp"),
        P(("fsdp", "tp")),
        P(("fsdp", "tp")),
        P(("fsdp", "tp")),
        P("fsdp", "tp"),
        P("tp", "fsdp"),
        P("tp", "fsdp"),
        P(("fsdp", "tp")),
        P(("fsdp", "tp")),
        P(("fsdp", "tp")),
        P(None, "fsdp", None),
        P(None, ("fsdp", "tp"), None),
    )
    out_specs = (
        P(None, ("fsdp", "tp"), None),
        P(None, ("fsdp", "tp"), None),
        P("fsdp", "tp"),
        P("fsdp", "tp"),
        P("fsdp", "tp"),
        P("tp", "fsdp"),
        P("tp", "fsdp"),
        P("tp", "fsdp"),
        P(("fsdp", "tp")),
        P(("fsdp", "tp")),
        P(("fsdp", "tp")),
        P("fsdp", "tp"),
        P("tp", "fsdp"),
        P("tp", "fsdp"),
        P(("fsdp", "tp")),
        P(("fsdp", "tp")),
        P(("fsdp", "tp")),
    )
    body = chip_shards if (mesh.shape["fsdp"], mesh.shape["tp"]) == (8, 4) else shards
    return jax.shard_map(body, mesh=mesh, in_specs=in_specs, out_specs=out_specs, check_vma=False)
```
